512 devices in a mesh: dp: 32 (over z, core), cls: 16 (over y, x).
Axes of the slice: x: 4, y: 4, z: 16, core: 2. Of those that a mesh axis runs over, the one named last changes fastest.
Arguments:
- attended: bfloat16 [442368, 1024], P(('dp', 'cls')), may hold values from -6 to 6
- stream: bfloat16 [442368, 1024], P(('dp', 'cls')), may hold values from -6 to 6
- out_proj: bfloat16 [1024, 1024], P('dp'), may hold values from -0.1875 to 0.1875
- norm_gain: float32 [1024], replicated, may hold values from 0.25 to 1.75
- norm_shift: float32 [1024], replicated, may hold values from -0.75 to 0.75
- head_proj: bfloat16 [1024, 512], P('dp'), may hold values from -0.1875 to 0.1875
- class_weight: bfloat16 [16384, 512], P('cls'), may hold values from -6 to 6
- block_ids: int32 [32, 16, 3], P('dp', 'cls'), may hold values from 0 to 7, as said below
- block_count: int32 [32, 16], P('dp', 'cls'), may hold values from 1 to 3, as said below
- labels: int32 [3072], P('dp'), may hold values from 0 to 16383, as said below
Outputs:
- sample_loss: float32 [3072], P(('dp', 'cls'))
- embed_grad: float32 [3072, 512], P(('dp', 'cls'))
- class_grad: float32 [16384, 512], P('cls', 'dp')
The draws below stay inside these ranges and needn't reach their ends.
Inputs may be any that keep to these rules, and one draw needn't show every extreme that they name: `block_ids`: within one data group and class shard the 3 block numbers are all different. `block_count`: some data group and class shard has all 3 slots live, another just one. `labels`: every image's class lies in a live slot's block of its own data group.
All inputs are finite; a program needn't handle non-finite values.
Results may differ from the reference program's by a relative error of at most 0.0028.
Values may be sent and summed in bfloat16 or wider, within the bound.
A program may use at most 64 MiB of HBM per device.

```python
import math
from functools import partial
import jax
import jax.numpy as jnp
from jax import lax

D = 1024
E = 512
P_SIZE = 144
BLOCK_ROWS = 128
BLOCKS_DEV = 8
SLOTS = 3
CLS_DEV = 1024
CLASSES = 16384
GROUP = 96
IMAGES = 3072
N_DP = 32
N_CLS = 16


def sample_plan(key):
    subkeys = jax.random.split(jax.random.fold_in(key, 11), 7)
    scores = jax.random.randint(subkeys[0], (N_DP, N_CLS, BLOCKS_DEV), 0, 1 << 20) * BLOCKS_DEV + jnp.arange(BLOCKS_DEV, dtype=jnp.int32)
    ranking = jnp.argsort(scores, axis=-1, stable=True)
    slot_ids = ranking[:, :, :SLOTS].astype(jnp.int32)
    pairs = N_DP * N_CLS
    counts = jax.random.randint(subkeys[1], (pairs,), 1, SLOTS + 1)
    full_at = jax.random.randint(subkeys[2], (), 0, pairs)
    single_at = (full_at + 1 + jax.random.randint(subkeys[3], (), 0, pairs - 1)) % pairs
    counts = counts.at[full_at].set(SLOTS).at[single_at].set(1).reshape(N_DP, N_CLS).astype(jnp.int32)
    group_of = jnp.arange(IMAGES, dtype=jnp.int32) // GROUP
    shard_pick = jax.random.randint(subkeys[4], (IMAGES,), 0, N_CLS)
    slot_pick = jax.random.randint(subkeys[5], (IMAGES,), 0, 1 << 20) % counts[group_of, shard_pick]
    row_pick = jax.random.randint(subkeys[6], (IMAGES,), 0, BLOCK_ROWS)
    block_pick = slot_ids[group_of, shard_pick, slot_pick]
    target = shard_pick * (BLOCKS_DEV * BLOCK_ROWS) + block_pick * BLOCK_ROWS + row_pick
    return (slot_ids, counts, target.astype(jnp.int32))


def draw_block_ids(key, part):
    return sample_plan(key)[0]


def draw_block_count(key, part):
    return sample_plan(key)[1]


def draw_labels(key, part):
    return sample_plan(key)[2]


def levels(stream_key, shape, pieces, low, largest):
    def one(axis_at, shards_of):
        draws = jax.random.uniform(jax.random.fold_in(jax.random.fold_in(stream_key, 6), axis_at), (shards_of,), jnp.float32, low / len(pieces), largest / len(pieces))
        return jnp.repeat(jnp.exp(draws), shape[axis_at] // shards_of).reshape((-1,) + (1,) * (len(shape) - axis_at - 1))

    level = one(*pieces[0])
    for cut in pieces[1:]:
        level = level * one(*cut)
    return level


def noise(stream_key, extent, width, bound, cuts=(), kind=jnp.bfloat16):
    drawn = width * jax.random.normal(stream_key, extent, jnp.float32)
    if cuts:
        drawn = drawn * levels(stream_key, extent, cuts, -0.22, 0.18)
    return jnp.clip(drawn, -bound, bound).astype(kind)


def setup_inputs(seed: int = 0) -> dict:
    arg_keys = jax.random.split(jax.random.key(seed), 11)
    attended = noise(arg_keys[0], (IMAGES * P_SIZE, D), 1.0, 6.0, ((0, 512),))
    stream = noise(arg_keys[1], (IMAGES * P_SIZE, D), 1.0, 6.0, ((0, 512),))
    out_proj = noise(arg_keys[2], (D, D), D ** -0.5, 0.1875, ((0, 32),))
    norm_gain = jnp.clip(1.0 + 0.15 * jax.random.normal(arg_keys[3], (D,), jnp.float32), 0.25, 1.75)
    norm_shift = noise(arg_keys[4], (D,), 0.05, 0.75, (), jnp.float32)
    head_proj = noise(arg_keys[5], (D, E), D ** -0.5, 0.1875, ((0, 32),))
    class_weight = noise(arg_keys[6], (CLASSES, E), 1.0, 6.0, ((0, 16),))
    block_ids = draw_block_ids(jax.random.fold_in(arg_keys[10], 71), 0)
    block_count = draw_block_count(jax.random.fold_in(arg_keys[10], 71), 0)
    labels = draw_labels(jax.random.fold_in(arg_keys[10], 71), 0)
    return dict(attended=attended, stream=stream, out_proj=out_proj, norm_gain=norm_gain, norm_shift=norm_shift, head_proj=head_proj, class_weight=class_weight, block_ids=block_ids, block_count=block_count, labels=labels)


LOGIT_SCALE = 64.0
ANGLE_MARGIN = 0.5
NORM_EPSILON = 1e-06

def pool_group(group_tokens, out_proj, norm_gain, norm_shift):
    attended, stream = group_tokens
    mixed = stream.astype(jnp.float32) + jnp.dot(attended, out_proj, preferred_element_type=jnp.float32)
    token_mean = lax.optimization_barrier(jnp.mean(mixed, axis=1, keepdims=True))
    centred = mixed - token_mean
    variance = lax.optimization_barrier(jnp.mean(centred * centred, axis=1, keepdims=True))
    normed = norm_gain * centred / jnp.sqrt(variance + NORM_EPSILON) + norm_shift
    return lax.optimization_barrier(jnp.mean(normed.reshape(GROUP, P_SIZE, D), axis=1)).astype(jnp.bfloat16)

def reference(attended, stream, out_proj, norm_gain, norm_shift, head_proj, class_weight, block_ids, block_count, labels):
    pooled = lax.map(partial(pool_group, out_proj=out_proj, norm_gain=norm_gain, norm_shift=norm_shift), (attended.reshape(N_DP, GROUP * P_SIZE, D), stream.reshape(N_DP, GROUP * P_SIZE, D)))
    pooled = pooled.reshape(IMAGES, D)
    embedding = jnp.dot(pooled, head_proj, preferred_element_type=jnp.float32)
    embed_norm = jnp.sqrt(lax.optimization_barrier(jnp.sum(embedding * embedding, axis=1)) + NORM_EPSILON)
    unit_embed = embedding / embed_norm[:, None]
    weight_blocks = class_weight.reshape(N_CLS, BLOCKS_DEV, BLOCK_ROWS, E)
    shard_range = jnp.arange(N_CLS, dtype=jnp.int32)
    slot_range = jnp.arange(SLOTS, dtype=jnp.int32)
    row_range = jnp.arange(BLOCK_ROWS, dtype=jnp.int32)
    block_range = jnp.arange(BLOCKS_DEV, dtype=jnp.int32)

    def step_group(dense_total, group_data):
        unit_group, norm_group, slot_ids, live_count, group_labels = group_data
        picked = weight_blocks[shard_range[:, None], slot_ids].astype(jnp.float32).reshape(-1, E)
        weight_norm = jnp.sqrt(lax.optimization_barrier(jnp.sum(picked * picked, axis=1)) + NORM_EPSILON)
        unit_weight = picked / weight_norm[:, None]
        cosine = jnp.dot(unit_group, unit_weight.T, precision=lax.Precision.HIGHEST, preferred_element_type=jnp.float32)
        slot_live = slot_range[None, :] < live_count[:, None]
        live_mask = jnp.broadcast_to(slot_live[:, :, None], (N_CLS, SLOTS, BLOCK_ROWS)).reshape(-1)
        column_class = (shard_range[:, None, None] * CLS_DEV + slot_ids[:, :, None] * BLOCK_ROWS + row_range[None, None, :]).reshape(-1)
        target_mask = (column_class[None, :] == group_labels[:, None]) & live_mask[None, :]
        target_cos = cosine * math.cos(ANGLE_MARGIN) - jnp.sqrt(1.0 - cosine * cosine) * math.sin(ANGLE_MARGIN)
        logits = LOGIT_SCALE * jnp.where(target_mask, target_cos, cosine)
        exponent = jnp.where(live_mask[None, :], jnp.exp(logits - LOGIT_SCALE), 0.0)
        denominator = lax.optimization_barrier(jnp.sum(exponent, axis=1))
        target_logit = lax.optimization_barrier(jnp.sum(jnp.where(target_mask, logits, 0.0), axis=1))
        sample_loss = jnp.log(denominator) + LOGIT_SCALE - target_logit
        target_float = target_mask.astype(jnp.float32)
        cos_grad = LOGIT_SCALE * (exponent / denominator[:, None] - target_float)
        unit_grad = jnp.dot(cos_grad, unit_weight, precision=lax.Precision.HIGHEST, preferred_element_type=jnp.float32)
        embed_grad = (unit_grad - unit_group * lax.optimization_barrier(jnp.sum(unit_group * unit_grad, axis=1, keepdims=True))) / norm_group[:, None]
        weight_unit_grad = jnp.dot(cos_grad.T, unit_group, precision=lax.Precision.HIGHEST, preferred_element_type=jnp.float32)
        weight_grad = (weight_unit_grad - unit_weight * lax.optimization_barrier(jnp.sum(unit_weight * weight_unit_grad, axis=1, keepdims=True))) / weight_norm[:, None]
        placement = ((block_range[None, :, None] == slot_ids[:, None, :]) & slot_live[:, None, :]).astype(jnp.float32)
        dense_grad = jnp.einsum('cbk,ckx->cbx', placement, weight_grad.reshape(N_CLS, SLOTS, BLOCK_ROWS * E), precision=lax.Precision.HIGHEST)
        return (dense_total + dense_grad, (sample_loss, embed_grad))
    initial = jnp.zeros((N_CLS, BLOCKS_DEV, BLOCK_ROWS * E), jnp.float32)
    dense_total, outputs = lax.scan(step_group, initial, (unit_embed.reshape(N_DP, GROUP, E), embed_norm.reshape(N_DP, GROUP), block_ids, block_count, labels.reshape(N_DP, GROUP)))
    sample_loss, embed_grad = outputs
    return (sample_loss.reshape(IMAGES), embed_grad.reshape(IMAGES, E), dense_total.reshape(CLASSES, E))
```

```python
import functools
import math

import jax
import jax.numpy as jnp
from jax import lax
from jax.experimental import pallas as pl
from jax.experimental.pallas import tpu as pltpu
from jax.sharding import PartitionSpec as P

P_SIZE = 144
BLOCK_ROWS = 128
LOGIT_SCALE = 64.0
ANGLE_MARGIN = 0.5
NORM_EPSILON = 1e-06
LANES = 128
PAD = 8

MESH = pl.DeviceIdType.MESH
VMEM = pl.BlockSpec(memory_space=pltpu.VMEM)
HBM = pl.BlockSpec(memory_space=pltpu.HBM)


def remote(src, dst, send, recv, device):
    return pltpu.make_async_remote_copy(
        src_ref=src,
        dst_ref=dst,
        send_sem=send,
        recv_sem=recv,
        device_id=device,
        device_id_type=MESH,
    )


def split(x):
    high = x.astype(jnp.bfloat16)
    low = (x - high.astype(jnp.float32)).astype(jnp.bfloat16)
    return high, low


def dot3(a, b, contract=((1,), (0,))):
    (ah, al), (bh, bl) = a, b
    dims = (contract, ((), ()))
    mul = functools.partial(
        lax.dot_general, dimension_numbers=dims, preferred_element_type=jnp.float32
    )
    return mul(ah, bh) + (mul(ah, bl) + mul(al, bh))


def gather_kernel(chips, op_ref, hp_ref, w_ref, h_ref, ring_s, ring_r, sib_s, sib_r, own_sem):
    dp, cls = lax.axis_index("dp"), lax.axis_index("cls")
    z, core = dp // 2, dp % 2
    right = lax.rem(z + 1, chips) * 2 + core
    left = lax.rem(z + chips - 1, chips) * 2 + core
    sibling = z * 2 + 1 - core
    half = op_ref.shape[0] // 2
    own = []
    for i, (src, dst) in enumerate(((op_ref, w_ref), (hp_ref, h_ref))):
        rows = pl.ds(pl.multiple_of(dp * 2 * half, 2 * half), 2 * half)
        own.append(pltpu.make_async_copy(src, dst.at[rows], own_sem.at[i]))
        own[-1].start()
    barrier = pltpu.get_barrier_semaphore()
    for peer in (left, right, sibling):
        pl.semaphore_signal(barrier, inc=1, device_id=(peer, cls), device_id_type=MESH)
    pl.semaphore_wait(barrier, 3)
    for copy in own:
        copy.wait()

    items = ((w_ref, 0), (w_ref, 1), (h_ref, 0), (h_ref, 1))
    far = chips // 2

    def rows_of(ref, part, chip, k):
        start = pl.multiple_of((chip * 2 + k) * (2 * half) + part * half, half)
        return ref.at[pl.ds(start, half)]

    def ring(item, way, step):
        ref, part = items[item]
        chip = lax.rem(z - (step - 1) + chips, chips) if way == 0 else lax.rem(z + step - 1, chips)
        block = rows_of(ref, part, chip, core)
        peer = right if way == 0 else left
        return remote(
            block, block, ring_s.at[way, step - 1, item], ring_r.at[way, step - 1, item], (peer, cls)
        )

    def arrival(item, way, step):
        ref, part = items[item]
        chip = lax.rem(z - step + chips, chips) if way == 0 else lax.rem(z + step, chips)
        block = rows_of(ref, part, chip, core)
        return remote(
            block,
            block,
            ring_s.at[way, step - 1, item],
            ring_r.at[way, step - 1, item],
            (right if way == 0 else left, cls),
        )

    def goes(item, way, step):
        return step < far or (step == far and items[item][1] == way)

    def hand(item, way, step):
        ref, part = items[item]
        chip = lax.rem(z - step + chips, chips) if way == 0 else lax.rem(z + step, chips)
        block = rows_of(ref, part, chip, core)
        return remote(
            block, block, sib_s.at[way, step, item], sib_r.at[way, step, item], (sibling, cls)
        )

    def taken(item, way, step):
        ref, part = items[item]
        chip = lax.rem(z - step + chips, chips) if way == 0 else lax.rem(z + step, chips)
        block = rows_of(ref, part, chip, 1 - core)
        return remote(
            block, block, sib_s.at[way, step, item], sib_r.at[way, step, item], (sibling, cls)
        )

    sent, handed = [], []
    for item in range(len(items)):
        for way in (0, 1):
            sent.append(ring(item, way, 1))
            sent[-1].start()
        handed.append((item, 0, 0))
        hand(item, 0, 0).start()
    for step in range(1, far + 1):
        for item in range(len(items)):
            for way in (0, 1):
                if not goes(item, way, step):
                    continue
                arrival(item, way, step).wait_recv()
                if goes(item, way, step + 1):
                    sent.append(ring(item, way, step + 1))
                    sent[-1].start()
                handed.append((item, way, step))
                hand(item, way, step).start()
    for key in handed:
        taken(*key).wait_recv()
    for copy in sent:
        copy.wait_send()
    for key in handed:
        hand(*key).wait_send()


def gather(chips, out_proj, head_proj):
    n_dp = 2 * chips
    w_rows, width = out_proj.shape
    h_rows, embed = head_proj.shape
    far = chips // 2
    return pl.pallas_call(
        functools.partial(gather_kernel, chips),
        name="gather_rows",
        out_shape=(
            jax.ShapeDtypeStruct((n_dp * w_rows, width), out_proj.dtype),
            jax.ShapeDtypeStruct((n_dp * h_rows, embed), head_proj.dtype),
        ),
        in_specs=[HBM, HBM],
        out_specs=(VMEM, VMEM),
        scratch_shapes=[
            pltpu.SemaphoreType.DMA((2, far, 4)),
            pltpu.SemaphoreType.DMA((2, far, 4)),
            pltpu.SemaphoreType.DMA((2, far + 1, 4)),
            pltpu.SemaphoreType.DMA((2, far + 1, 4)),
            pltpu.SemaphoreType.DMA((2,)),
        ],
        compiler_params=pltpu.CompilerParams(
            collective_id=0, has_side_effects=True, vmem_limit_bytes=4 << 20
        ),
        cost_estimate=pl.CostEstimate(
            flops=40_000_000_000, bytes_accessed=20 << 20, transcendentals=0
        ),
    )(out_proj, head_proj)


def main_kernel(
    n_dp,
    n_cls,
    images,
    att,
    stream,
    w,
    head,
    weight,
    gain_ref,
    shift_ref,
    slots_ref,
    label_ref,
    loss_ref,
    egrad_ref,
    cgrad_ref,
    mixed,
    pooled_own,
    pooled_all,
    unit_w,
    unit_wt,
    norm_w,
    ids_own,
    ids_all,
    soft_own,
    soft_all,
    eg_own,
    eg_all,
    wg_own,
    wg_all,
    pool_s,
    pool_r,
    ids_s,
    ids_r,
    soft_s,
    soft_r,
    eg_s,
    eg_r,
    wg_s,
    wg_r,
):
    f32 = jnp.float32
    dp, cls = lax.axis_index("dp"), lax.axis_index("cls")
    chips = n_dp // 2
    z, core = dp // 2, dp % 2
    slots = slots_ref.shape[1] - 1
    embed = head.shape[1]
    columns = slots * BLOCK_ROWS
    cls_dev = weight.shape[0]
    blocks_dev = cls_dev // BLOCK_ROWS

    barrier = pltpu.get_barrier_semaphore()
    for off in range(1, n_cls):
        peer = (dp, lax.rem(cls + off, n_cls))
        pl.semaphore_signal(barrier, inc=1, device_id=peer, device_id_type=MESH)
    for off in range(1, n_dp):
        peer = (lax.rem(dp + off, n_dp), cls)
        pl.semaphore_signal(barrier, inc=1, device_id=peer, device_id_type=MESH)

    row8 = lax.broadcasted_iota(jnp.int32, (PAD, LANES), 0)
    slot = [slots_ref[0:1, k : k + 1] for k in range(slots)]
    count = slots_ref[0:1, slots : slots + 1]
    numbers = jnp.full((PAD, LANES), -1, jnp.int32)
    for k in range(slots):
        kept = (row8 == k) & (jnp.broadcast_to(count, row8.shape) > k)
        numbers = jnp.where(kept, jnp.broadcast_to(slot[k], row8.shape), numbers)
    ids_own[...] = numbers

    spread_from = lax.broadcasted_iota(jnp.int32, (images * n_cls, LANES), 0)
    spread_to = lax.broadcasted_iota(jnp.int32, (images * n_cls, LANES), 1)
    spread = ((spread_from // images) * PAD + spread_from % images == spread_to).astype(f32)
    labels = jnp.dot(
        jnp.broadcast_to(label_ref[...].astype(f32) + 1.0, (PAD, images * n_cls)),
        spread,
        precision=lax.Precision.HIGHEST,
        preferred_element_type=f32,
    )[0:1]

    mixed[...] = jnp.dot(att[...], w[...], preferred_element_type=f32)
    pooled_own[...] = jnp.zeros_like(pooled_own)
    rows = []
    for i in range(images):
        token = pl.ds(i * P_SIZE, P_SIZE)
        value = mixed[token] + stream[token].astype(f32)
        centred = value - jnp.mean(value, axis=1, keepdims=True)
        variance = jnp.mean(centred * centred, axis=1, keepdims=True)
        scaled = centred / jnp.sqrt(variance + NORM_EPSILON)
        rows.append(jnp.sum(scaled, axis=0, keepdims=True))
    rows.append(jnp.zeros((PAD - images, rows[0].shape[1]), f32))
    pooled = gain_ref[...] * (jnp.concatenate(rows, axis=0) * (1.0 / P_SIZE)) + shift_ref[...]
    real = lax.broadcasted_iota(jnp.int32, pooled.shape, 0) < images
    pooled = jnp.where(real, pooled, 0.0).astype(jnp.bfloat16)
    pooled_own[...] = pooled
    pooled_all[cls] = pooled

    pl.semaphore_wait(barrier, n_cls - 1 + n_dp - 1)

    def plane(off):
        return (dp, lax.rem(cls + off, n_cls))

    def pool_copy(off):
        return remote(
            pooled_own, pooled_all.at[cls], pool_s.at[off], pool_r.at[off], plane(off)
        )

    def pool_taken(off):
        source = lax.rem(cls - off + n_cls, n_cls)
        return remote(
            pooled_own, pooled_all.at[source], pool_s.at[off], pool_r.at[off], plane(off)
        )

    for off in range(1, n_cls):
        pool_copy(off).start()

    def column(off):
        chip, other = off // 2, off % 2
        return (lax.rem(z + chip, chips) * 2 + lax.rem(core + other, 2), cls)

    def ids_copy(off):
        return remote(ids_own, ids_all.at[off], ids_s.at[off], ids_r.at[off], column(off))

    order = sorted(range(1, n_dp), key=lambda off: -min(off // 2, chips - off // 2))
    for off in order:
        ids_copy(off).start()

    for k in range(slots):
        row = lax.broadcasted_iota(jnp.int32, (BLOCK_ROWS, cls_dev), 0)
        chosen = row + jnp.broadcast_to(slot[k] * BLOCK_ROWS, row.shape)
        pick = lax.broadcasted_iota(jnp.int32, row.shape, 1) == chosen
        pick = jnp.where(pick, 1.0, 0.0).astype(jnp.bfloat16)
        block = jnp.dot(pick, weight[...], preferred_element_type=f32)
        span = pl.ds(k * BLOCK_ROWS, BLOCK_ROWS)
        norm = jnp.sqrt(jnp.sum(block * block, axis=1, keepdims=True) + NORM_EPSILON)
        unit_w[span] = block / norm
        turned = block.T
        norm_row = jnp.sqrt(jnp.sum(turned * turned, axis=0, keepdims=True) + NORM_EPSILON)
        unit_wt[:, span] = turned / norm_row
        norm_w[:, span] = jnp.broadcast_to(norm_row, (PAD, BLOCK_ROWS))
    uw = split(unit_w[...])

    own_embed = jnp.dot(
        jnp.concatenate([pooled.astype(f32), jnp.zeros_like(pooled, f32)]).astype(jnp.bfloat16),
        head[...],
        preferred_element_type=f32,
    )[:PAD]
    own_norm = jnp.sqrt(jnp.sum(own_embed * own_embed, axis=1, keepdims=True) + NORM_EPSILON)
    own_unit = own_embed / own_norm

    for off in range(1, n_cls):
        pool_taken(off).wait_recv()
    group = pooled_all[...].astype(f32).reshape(n_cls * PAD, -1).astype(jnp.bfloat16)
    embedding = jnp.dot(group, head[...], preferred_element_type=f32).T
    embed_norm = jnp.sqrt(jnp.sum(embedding * embedding, axis=0, keepdims=True) + NORM_EPSILON)
    unit = split(embedding / embed_norm)

    cosine = dot3(uw, unit)
    classes, alive = [], []
    for k in range(slots):
        row = lax.broadcasted_iota(jnp.int32, (BLOCK_ROWS, LANES), 0)
        number = row + jnp.broadcast_to(slot[k] * BLOCK_ROWS, row.shape) + (cls * cls_dev + 1)
        live = jnp.broadcast_to(count, row.shape) > k
        alive.append(jnp.where(live, 1.0, 0.0))
        classes.append(jnp.where(live, number.astype(f32), -1.0))
    classes, alive = jnp.concatenate(classes, axis=0), jnp.concatenate(alive, axis=0)
    target = classes == labels
    target_cos = cosine * math.cos(ANGLE_MARGIN) - jnp.sqrt(1.0 - cosine * cosine) * math.sin(
        ANGLE_MARGIN
    )
    logits = LOGIT_SCALE * jnp.where(target, target_cos, cosine)
    exponent = jnp.where(alive > 0.0, jnp.exp(logits - LOGIT_SCALE), 0.0)
    denom_part = jnp.sum(exponent, axis=0, keepdims=True)
    target_part = jnp.sum(jnp.where(target, logits, 0.0), axis=0, keepdims=True)
    soft = jnp.where(row8 == 0, denom_part, jnp.where(row8 == 1, target_part, 0.0))
    soft_own[...] = soft
    soft_all[0] = soft

    def soft_copy(off):
        return remote(soft_own, soft_all.at[off], soft_s.at[off], soft_r.at[off], plane(off))

    for off in range(1, n_cls):
        soft_copy(off).start()
    for off in range(1, n_cls):
        soft_copy(off).wait_recv()
    total = jnp.sum(soft_all[...], axis=0)
    denominator, target_logit = total[0:1], total[1:2]

    cos_grad = LOGIT_SCALE * (exponent / denominator - jnp.where(target, 1.0, 0.0))
    cg = split(cos_grad)
    along = jnp.dot(
        jnp.ones((PAD, LANES), f32),
        (cos_grad * cosine).T,
        precision=lax.Precision.HIGHEST,
        preferred_element_type=f32,
    )[0:1]
    weight_unit_grad = dot3(unit, cg, ((1,), (1,)))
    weight_grad = (weight_unit_grad - unit_wt[...] * along) / norm_w[0:1]
    wg_own[...] = weight_grad.astype(jnp.bfloat16)
    cut = embed // n_dp

    def grad_copy(off):
        peer = column(off)
        rows_for = pl.ds(pl.multiple_of(peer[0] * cut, cut), cut)
        return remote(wg_own.at[rows_for], wg_all.at[off], wg_s.at[off], wg_r.at[off], peer)

    for off in order:
        grad_copy(off).start()

    part = dot3(split(cos_grad.T), uw)
    eg_own[...] = part.reshape(n_cls, PAD, embed)
    eg_all[0] = eg_own[cls]

    def eg_copy(off):
        peer = plane(off)
        return remote(eg_own.at[peer[1]], eg_all.at[off], eg_s.at[off], eg_r.at[off], peer)

    for off in range(1, n_cls):
        eg_copy(off).start()
    loss = jnp.log(denominator) + LOGIT_SCALE - target_logit
    lane8 = lax.broadcasted_iota(jnp.int32, (PAD, LANES), 1)
    mine = jnp.where(lane8 == row8 + cls * PAD, loss, 0.0)
    loss_ref[...] = jnp.broadcast_to(jnp.sum(mine, axis=1, keepdims=True), (PAD, LANES))
    for off in range(1, n_cls):
        eg_copy(off).wait_recv()
    unit_grad = jnp.sum(eg_all[...], axis=0)
    egrad_ref[...] = (
        unit_grad - own_unit * jnp.sum(own_unit * unit_grad, axis=1, keepdims=True)
    ) / own_norm

    sums = [jnp.zeros((cut, BLOCK_ROWS), f32) for _ in range(blocks_dev)]
    own_rows = pl.ds(pl.multiple_of(dp * cut, cut), cut)
    for off in [0] + order[::-1]:
        if off:
            ids_copy(off).wait_recv()
            grad_copy(off).wait_recv()
        for k in range(slots):
            span = pl.ds(k * BLOCK_ROWS, BLOCK_ROWS)
            if off:
                value, number = wg_all[off, :, span], ids_all[off, k : k + 1]
            else:
                value, number = wg_own[own_rows, span], ids_own[k : k + 1]
            value = value.astype(f32)
            number = jnp.broadcast_to(number, value.shape)
            for b in range(blocks_dev):
                sums[b] = sums[b] + jnp.where(number == b, value, 0.0)
    for b in range(blocks_dev):
        cgrad_ref[:, pl.ds(b * BLOCK_ROWS, BLOCK_ROWS)] = sums[b]

    for off in range(1, n_cls):
        pool_copy(off).wait_send()
        soft_copy(off).wait_send()
        eg_copy(off).wait_send()
    for off in order:
        ids_copy(off).wait_send()
        grad_copy(off).wait_send()


def per_device(
    n_dp,
    n_cls,
    attended,
    stream,
    out_proj,
    norm_gain,
    norm_shift,
    head_proj,
    class_weight,
    block_ids,
    block_count,
    labels,
):
    f32, bf16, i32 = jnp.float32, jnp.bfloat16, jnp.int32
    tokens, width = attended.shape
    images = tokens // P_SIZE
    embed = head_proj.shape[1]
    slots = block_ids.shape[2]
    columns = slots * BLOCK_ROWS
    cut = embed // n_dp
    dma = pltpu.SemaphoreType.DMA
    w, head = gather(n_dp // 2, out_proj, head_proj)
    loss, egrad, cgrad = pl.pallas_call(
        functools.partial(main_kernel, n_dp, n_cls, images),
        name="margin_softmax",
        out_shape=(
            jax.ShapeDtypeStruct((PAD, LANES), f32),
            jax.ShapeDtypeStruct((PAD, embed), f32),
            jax.ShapeDtypeStruct((cut, class_weight.shape[0]), f32),
        ),
        in_specs=[VMEM] * 9,
        out_specs=(VMEM, VMEM, VMEM),
        scratch_shapes=[
            pltpu.VMEM((tokens, width), f32),
            pltpu.VMEM((PAD, width), bf16),
            pltpu.VMEM((n_cls, PAD, width), bf16),
            pltpu.VMEM((columns, embed), f32),
            pltpu.VMEM((embed, columns), f32),
            pltpu.VMEM((PAD, columns), f32),
            pltpu.VMEM((PAD, LANES), i32),
            pltpu.VMEM((n_dp, PAD, LANES), i32),
            pltpu.VMEM((PAD, LANES), f32),
            pltpu.VMEM((n_cls, PAD, LANES), f32),
            pltpu.VMEM((n_cls, PAD, embed), f32),
            pltpu.VMEM((n_cls, PAD, embed), f32),
            pltpu.VMEM((embed, columns), bf16),
            pltpu.VMEM((n_dp, cut, columns), bf16),
            dma((n_cls,)),
            dma((n_cls,)),
            dma((n_dp,)),
            dma((n_dp,)),
            dma((n_cls,)),
            dma((n_cls,)),
            dma((n_cls,)),
            dma((n_cls,)),
            dma((n_dp,)),
            dma((n_dp,)),
        ],
        compiler_params=pltpu.CompilerParams(
            collective_id=1, has_side_effects=True, vmem_limit_bytes=32 << 20
        ),
    )(
        attended,
        stream,
        w,
        head,
        class_weight,
        norm_gain.reshape(1, width),
        norm_shift.reshape(1, width),
        jnp.concatenate([block_ids.reshape(1, slots), block_count], axis=1),
        labels.reshape(1, -1),
    )
    return loss[:images, 0], egrad[:images], cgrad.T


def solution(mesh):
    n_dp, n_cls = mesh.shape["dp"], mesh.shape["cls"]
    placed = (
        P(("dp", "cls"), None),
        P(("dp", "cls"), None),
        P("dp", None),
        P(),
        P(),
        P("dp", None),
        P("cls", None),
        P("dp", "cls", None),
        P("dp", "cls"),
        P("dp"),
    )
    return jax.shard_map(
        functools.partial(per_device, n_dp, n_cls),
        mesh=mesh,
        in_specs=placed,
        out_specs=(P(("dp", "cls")), P(("dp", "cls"), None), P("cls", "dp")),
        check_vma=False,
    )
```

```python
import functools
import math

import jax
import jax.numpy as jnp
from jax import lax
from jax.experimental import pallas as pl
from jax.experimental.pallas import tpu as pltpu
from jax.sharding import PartitionSpec as P

P_SIZE = 144
BLOCK_ROWS = 128
LOGIT_SCALE = 64.0
ANGLE_MARGIN = 0.5
NORM_EPSILON = 1e-06
LANES = 128
PAD = 8

MESH = pl.DeviceIdType.MESH
VMEM = pl.BlockSpec(memory_space=pltpu.VMEM)
SMEM = pl.BlockSpec(memory_space=pltpu.SMEM)
HBM = pl.BlockSpec(memory_space=pltpu.HBM)


def remote(src, dst, send, recv, device):
    return pltpu.make_async_remote_copy(
        src_ref=src,
        dst_ref=dst,
        send_sem=send,
        recv_sem=recv,
        device_id=device,
        device_id_type=MESH,
    )


def split(x):
    high = x.astype(jnp.bfloat16)
    low = (x - high.astype(jnp.float32)).astype(jnp.bfloat16)
    return high, low


def dot3(a, b, contract=((1,), (0,))):
    (ah, al), (bh, bl) = a, b
    dims = (contract, ((), ()))
    mul = functools.partial(
        lax.dot_general, dimension_numbers=dims, preferred_element_type=jnp.float32
    )
    return mul(ah, bh) + (mul(ah, bl) + mul(al, bh))


SIDE = 4
LEAPS = (6, -6, 3, -3)
RELAY = 4


def gather_kernel(chips, op_ref, hp_ref, wh_ref, own_sem, line_s, line_r, plane_s, plane_r, sib_s, sib_r):
    dp, cls = lax.axis_index("dp"), lax.axis_index("cls")
    z, core = dp // 2, dp % 2
    x, y = cls % SIDE, cls // SIDE
    shard, total = op_ref.shape[0], wh_ref.shape[1]
    width = op_ref.shape[1]
    half, wide = shard // 2, total // 2
    colour = (x + 2 * y) % SIDE
    sibling = (z * 2 + 1 - core, cls)

    def along(off):
        return (((z + off + chips) % chips) * 2 + core, cls)

    plane = [
        (dp, y * SIDE + (x + 1) % SIDE),
        (dp, y * SIDE + (x + SIDE - 1) % SIDE),
        (dp, ((y + 1) % SIDE) * SIDE + x),
        (dp, ((y + SIDE - 1) % SIDE) * SIDE + x),
    ]
    mine = pl.ds(pl.multiple_of(dp * shard, shard), shard)
    own = [
        pltpu.make_async_copy(op_ref, wh_ref.at[mine, pl.ds(0, width)], own_sem.at[0]),
        pltpu.make_async_copy(hp_ref, wh_ref.at[mine, pl.ds(width, total - width)], own_sem.at[1]),
    ]
    for copy in own:
        copy.start()
    barrier = pltpu.get_barrier_semaphore()
    line = [along(off) for off in (1, -1, 2, -2, *LEAPS)]
    for peer in (*line, sibling, *plane):
        pl.semaphore_signal(barrier, inc=1, device_id=peer, device_id_type=MESH)
    pl.semaphore_wait(barrier, len(line) + 5)
    for copy in own:
        copy.wait()

    def quarter(off, part=None):
        chip = (z - off + chips) % chips
        start = pl.multiple_of((chip * 2 + core) * shard + (colour // 2) * half, half)
        column = (colour % 2) * wide
        size = wide if part is None else wide // 2
        if part is not None:
            column = column + part * size
        return wh_ref.at[pl.ds(start, half), pl.ds(pl.multiple_of(column, LANES), size)]

    def count(rows, send, recv):
        block = wh_ref.at[pl.ds(0, rows)]
        return remote(block, block, send, recv, sibling)

    def pass_on(off, step):
        block = quarter(off)
        return remote(block, block, line_s, line_r.at[(off + step) % chips], along(step))

    def spread(off):
        block, arrived = quarter(off), plane_r.at[off % chips]
        for peer in plane[:2]:
            remote(block, block, plane_s, arrived, peer).start()
        for part, peer in enumerate(plane[2:]):
            piece = quarter(off, part)
            remote(piece, piece, plane_s, arrived, peer).start()

    def hand(off):
        start = pl.multiple_of(((z - off + chips) % chips * 2 + core) * shard, shard)
        block = wh_ref.at[pl.ds(start, shard)]
        remote(block, block, sib_s, sib_r, sibling).start()

    row_q = half // 2

    def taken(*offs):
        for off in offs:
            pass_on(off, 0).wait_recv()
            if off in LEAPS:
                pass_on(off, 1).start()
                pass_on(off, -1).start()
            if off == LEAPS[0]:
                pass_on(off, 2).start()
            spread(off)

    def complete(*offs):
        for off in offs:
            count(3 * row_q, plane_s, plane_r.at[off % chips]).wait_recv()
            hand(off)

    for step in (*LEAPS, 1, -1):
        pass_on(0, step).start()
    hand(0)
    taken(1, -1)
    taken(3, -3)
    complete(1, -1)
    taken(6, -6)
    complete(3, -3)
    taken(2, -2, 4, -4)
    complete(6, -6)
    taken(5, -5, 7, -7, 8)
    complete(2, -2, 4, -4)
    complete(5, -5, 7, -7, 8)
    others = chips - 1
    count(chips * shard, sib_s, sib_r).wait_recv()
    count(others * row_q, line_s, line_r.at[0]).wait_send()
    count(others * 3 * row_q, plane_s, plane_r.at[0]).wait_send()
    count(chips * shard, sib_s, sib_r).wait_send()


def gather(chips, out_proj, head_proj):
    shard, width = out_proj.shape
    embed = head_proj.shape[1]
    dma = pltpu.SemaphoreType.DMA
    return pl.pallas_call(
        functools.partial(gather_kernel, chips),
        name="gather_rows",
        out_shape=jax.ShapeDtypeStruct((2 * chips * shard, width + embed), out_proj.dtype),
        in_specs=[HBM, HBM],
        out_specs=VMEM,
        scratch_shapes=[dma((2,)), dma, dma((chips,)), dma, dma((chips,)), dma, dma],
        compiler_params=pltpu.CompilerParams(
            collective_id=0, has_side_effects=True, vmem_limit_bytes=4 << 20
        ),
        cost_estimate=pl.CostEstimate(
            flops=40_000_000_000, bytes_accessed=20 << 20, transcendentals=0
        ),
    )(out_proj, head_proj)


def main_kernel(
    n_dp,
    n_cls,
    images,
    att,
    stream,
    wh_ref,
    weight,
    gain_ref,
    shift_ref,
    ids_ref,
    count_ref,
    label_ref,
    loss_ref,
    egrad_ref,
    cgrad_ref,
    mixed,
    pooled_own,
    pooled_all,
    unit_w,
    unit_wt,
    norm_w,
    ids_own,
    ids_all,
    soft_own,
    soft_all,
    eg_own,
    eg_all,
    wg_own,
    wg_all,
    pool_s,
    pool_r,
    ids_s,
    ids_r,
    soft_s,
    soft_r,
    eg_s,
    eg_r,
    wg_s,
    wg_r,
    far_own,
    far_all,
    far_s,
    far_r,
):
    f32 = jnp.float32
    dp, cls = lax.axis_index("dp"), lax.axis_index("cls")
    chips = n_dp // 2
    z, core = dp // 2, dp % 2
    slots = ids_ref.shape[1]
    width = att.shape[1]
    embed = wh_ref.shape[1] - width
    columns = slots * BLOCK_ROWS
    cls_dev = weight.shape[0]
    blocks_dev = cls_dev // BLOCK_ROWS

    barrier = pltpu.get_barrier_semaphore()
    for off in range(1, n_cls):
        peer = (dp, lax.rem(cls + off, n_cls))
        pl.semaphore_signal(barrier, inc=1, device_id=peer, device_id_type=MESH)
    for off in range(1, n_dp):
        peer = (lax.rem(dp + off, n_dp), cls)
        pl.semaphore_signal(barrier, inc=1, device_id=peer, device_id_type=MESH)

    row8 = lax.broadcasted_iota(jnp.int32, (PAD, LANES), 0)
    slot = [ids_ref[0:1, k : k + 1] for k in range(slots)]
    count = jnp.full((1, LANES), count_ref[0, 0], jnp.int32)
    numbers = jnp.full((PAD, LANES), -1, jnp.int32)
    for k in range(slots):
        kept = (row8 == k) & (jnp.broadcast_to(count, row8.shape) > k)
        numbers = jnp.where(kept, jnp.broadcast_to(slot[k], row8.shape), numbers)
    ids_own[...] = numbers

    spread_from = lax.broadcasted_iota(jnp.int32, (images * n_cls, LANES), 0)
    spread_to = lax.broadcasted_iota(jnp.int32, (images * n_cls, LANES), 1)
    spread = ((spread_from // images) * PAD + spread_from % images == spread_to).astype(f32)
    labels = jnp.dot(
        jnp.broadcast_to(label_ref[...].astype(f32) + 1.0, (PAD, images * n_cls)),
        spread,
        precision=lax.Precision.HIGHEST,
        preferred_element_type=f32,
    )[0:1]

    mixed[...] = jnp.dot(att[...], wh_ref[:, :width], preferred_element_type=f32)
    pooled_own[...] = jnp.zeros_like(pooled_own)
    rows = []
    for i in range(images):
        token = pl.ds(i * P_SIZE, P_SIZE)
        value = mixed[token] + stream[token].astype(f32)
        centred = value - jnp.mean(value, axis=1, keepdims=True)
        variance = jnp.mean(centred * centred, axis=1, keepdims=True)
        scaled = centred / jnp.sqrt(variance + NORM_EPSILON)
        rows.append(jnp.sum(scaled, axis=0, keepdims=True))
    rows.append(jnp.zeros((PAD - images, rows[0].shape[1]), f32))
    pooled = gain_ref[...] * (jnp.concatenate(rows, axis=0) * (1.0 / P_SIZE)) + shift_ref[...]
    real = lax.broadcasted_iota(jnp.int32, pooled.shape, 0) < images
    pooled = jnp.where(real, pooled, 0.0).astype(jnp.bfloat16)
    pooled_own[...] = pooled
    pooled_all[cls] = pooled

    pl.semaphore_wait(barrier, n_cls - 1 + n_dp - 1)

    def plane(off):
        return (dp, lax.rem(cls + off, n_cls))

    def pool_copy(off):
        return remote(
            pooled_own, pooled_all.at[cls], pool_s, pool_r, plane(off)
        )

    def tally(ref, send, recv):
        block = ref.at[pl.ds(1, ref.shape[0] - 1)]
        return remote(block, block, send, recv, plane(1))

    for off in range(1, n_cls):
        pool_copy(off).start()

    def column(shift, other):
        return (((z + shift + chips) % chips) * 2 + (core + other) % 2, cls)

    near = [(s, o) for s in range(1 - RELAY, RELAY + 1) for o in (0, 1) if s or o]

    def ids_copy(shift, other):
        held = ids_all.at[2 * (shift % chips) + other]
        return remote(ids_own, held, ids_s, ids_r, column(shift, other))

    for shift, other in near:
        ids_copy(shift, other).start()

    for k in range(slots):
        row = lax.broadcasted_iota(jnp.int32, (BLOCK_ROWS, cls_dev), 0)
        chosen = row + jnp.broadcast_to(slot[k] * BLOCK_ROWS, row.shape)
        pick = lax.broadcasted_iota(jnp.int32, row.shape, 1) == chosen
        pick = jnp.where(pick, 1.0, 0.0).astype(jnp.bfloat16)
        block = jnp.dot(pick, weight[...], preferred_element_type=f32)
        span = pl.ds(k * BLOCK_ROWS, BLOCK_ROWS)
        norm = jnp.sqrt(jnp.sum(block * block, axis=1, keepdims=True) + NORM_EPSILON)
        unit_w[span] = block / norm
        turned = block.T
        norm_row = jnp.sqrt(jnp.sum(turned * turned, axis=0, keepdims=True) + NORM_EPSILON)
        unit_wt[:, span] = turned / norm_row
        norm_w[:, span] = jnp.broadcast_to(norm_row, (PAD, BLOCK_ROWS))
    uw = split(unit_w[...])

    head = wh_ref[:, width:]
    own_embed = jnp.dot(
        jnp.concatenate([pooled.astype(f32), jnp.zeros_like(pooled, f32)]).astype(jnp.bfloat16),
        head,
        preferred_element_type=f32,
    )[:PAD]
    own_norm = jnp.sqrt(jnp.sum(own_embed * own_embed, axis=1, keepdims=True) + NORM_EPSILON)
    own_unit = own_embed / own_norm

    tally(pooled_all, pool_s, pool_r).wait_recv()
    group = pooled_all[...].astype(f32).reshape(n_cls * PAD, -1).astype(jnp.bfloat16)
    embedding = jnp.dot(group, head, preferred_element_type=f32).T
    embed_norm = jnp.sqrt(jnp.sum(embedding * embedding, axis=0, keepdims=True) + NORM_EPSILON)
    unit = split(embedding / embed_norm)

    cosine = dot3(uw, unit)
    classes, alive = [], []
    for k in range(slots):
        row = lax.broadcasted_iota(jnp.int32, (BLOCK_ROWS, LANES), 0)
        number = row + jnp.broadcast_to(slot[k] * BLOCK_ROWS, row.shape) + (cls * cls_dev + 1)
        live = jnp.broadcast_to(count, row.shape) > k
        alive.append(jnp.where(live, 1.0, 0.0))
        classes.append(jnp.where(live, number.astype(f32), -1.0))
    classes, alive = jnp.concatenate(classes, axis=0), jnp.concatenate(alive, axis=0)
    target = classes == labels
    target_cos = cosine * math.cos(ANGLE_MARGIN) - jnp.sqrt(1.0 - cosine * cosine) * math.sin(
        ANGLE_MARGIN
    )
    logits = LOGIT_SCALE * jnp.where(target, target_cos, cosine)
    exponent = jnp.where(alive > 0.0, jnp.exp(logits - LOGIT_SCALE), 0.0)
    denom_part = jnp.sum(exponent, axis=0, keepdims=True)
    target_part = jnp.sum(jnp.where(target, logits, 0.0), axis=0, keepdims=True)
    soft = jnp.where(row8 == 0, denom_part, jnp.where(row8 == 1, target_part, 0.0))
    soft_own[...] = soft
    soft_all[0] = soft

    def soft_copy(off):
        return remote(soft_own, soft_all.at[off], soft_s, soft_r, plane(off))

    for off in range(1, n_cls):
        soft_copy(off).start()
    tally(soft_all, soft_s, soft_r).wait_recv()
    total = jnp.sum(soft_all[...], axis=0)
    denominator, target_logit = total[0:1], total[1:2]

    cos_grad = LOGIT_SCALE * (exponent / denominator - jnp.where(target, 1.0, 0.0))
    cg = split(cos_grad)
    along = jnp.dot(
        jnp.ones((PAD, LANES), f32),
        (cos_grad * cosine).T,
        precision=lax.Precision.HIGHEST,
        preferred_element_type=f32,
    )[0:1]
    weight_unit_grad = dot3(unit, cg, ((1,), (1,)))
    weight_grad = (weight_unit_grad - unit_wt[...] * along) / norm_w[0:1]
    wg_own[...] = weight_grad.astype(jnp.bfloat16)
    cut = embed // n_dp

    legs = [(s, o, RELAY) for s in range(RELAY, -1, -1) for o in (0, 1) if s or o]
    legs += [(-s, o, -RELAY) for s in range(RELAY - 1, -1, -1) for o in (0, 1) if s or o]
    legs += [(w * s, o, 0) for s in range(RELAY - 1, 0, -1) for w in (1, -1) for o in (0, 1)]
    legs += [(0, 1, 0)]

    def columns_of(chip, at):
        return pl.ds(pl.multiple_of((((chip + 2 * chips) % chips) * 2 + at) * cut, cut), cut)

    def leg_copy(t):
        shift, other, onward = legs[t]
        rows_for = columns_of(z + shift + onward, (core + other) % 2)
        return remote(wg_own.at[rows_for], wg_all.at[t], wg_s, wg_r.at[t], column(shift, other))

    for t in range(len(legs)):
        leg_copy(t).start()

    part = dot3(split(cos_grad.T), uw)
    eg_own[...] = part.reshape(n_cls, PAD, embed)
    eg_all[0] = eg_own[cls]

    def eg_copy(off):
        peer = plane(off)
        return remote(eg_own.at[peer[1]], eg_all.at[off], eg_s, eg_r, peer)

    for off in range(1, n_cls):
        eg_copy(off).start()
    loss = jnp.log(denominator) + LOGIT_SCALE - target_logit
    lane8 = lax.broadcasted_iota(jnp.int32, (PAD, LANES), 1)
    mine = jnp.where(lane8 == row8 + cls * PAD, loss, 0.0)
    loss_ref[...] = jnp.broadcast_to(jnp.sum(mine, axis=1, keepdims=True), (PAD, LANES))
    ids_got = ids_all.at[pl.ds(0, len(near))]
    remote(ids_got, ids_got, ids_s, ids_r, plane(1)).wait_recv()

    def add(sums, value, numbers):
        for k in range(slots):
            part = value[:, k * BLOCK_ROWS : (k + 1) * BLOCK_ROWS].astype(f32)
            number = jnp.broadcast_to(numbers[k : k + 1], part.shape)
            sums = [s + jnp.where(number == b, part, 0.0) for b, s in enumerate(sums)]
        return sums

    def gathered(onward):
        rows_for = columns_of(z + onward, core)
        sums = [jnp.zeros((cut, BLOCK_ROWS), f32) for _ in range(blocks_dev)]
        sums = add(sums, wg_own[rows_for], ids_own[...])
        for t in reversed(range(len(legs))):
            shift, other, onto = legs[t]
            if onto == onward:
                leg_copy(t).wait_recv()
                sums = add(sums, wg_all[t], ids_all[2 * (shift % chips) + other])
        return sums

    def relay_copy(way):
        to = column((-RELAY, RELAY)[way], 0)
        return remote(far_own.at[way], far_all.at[way], far_s, far_r.at[way], to)

    for way in (0, 1):
        for b, part in enumerate(gathered((-RELAY, RELAY)[way])):
            far_own[way, :, pl.ds(b * BLOCK_ROWS, BLOCK_ROWS)] = part.astype(jnp.bfloat16)
        relay_copy(way).start()

    tally(eg_all, eg_s, eg_r).wait_recv()
    unit_grad = jnp.sum(eg_all[...], axis=0)
    egrad_ref[...] = (
        unit_grad - own_unit * jnp.sum(own_unit * unit_grad, axis=1, keepdims=True)
    ) / own_norm

    sums = gathered(0)
    for way in (0, 1):
        relay_copy(way).wait_recv()
        sums = [
            s + far_all[way, :, pl.ds(b * BLOCK_ROWS, BLOCK_ROWS)].astype(f32)
            for b, s in enumerate(sums)
        ]
    for b in range(blocks_dev):
        cgrad_ref[:, pl.ds(b * BLOCK_ROWS, BLOCK_ROWS)] = sums[b]

    tally(pooled_all, pool_s, pool_r).wait_send()
    tally(soft_all, soft_s, soft_r).wait_send()
    tally(eg_all, eg_s, eg_r).wait_send()
    remote(ids_got, ids_got, ids_s, ids_r, plane(1)).wait_send()
    legs_sent = wg_all.at[pl.ds(0, len(legs))]
    remote(legs_sent, legs_sent, wg_s, wg_r.at[0], plane(1)).wait_send()
    remote(far_all, far_all, far_s, far_r.at[0], plane(1)).wait_send()


def per_device(
    n_dp,
    n_cls,
    attended,
    stream,
    out_proj,
    norm_gain,
    norm_shift,
    head_proj,
    class_weight,
    block_ids,
    block_count,
    labels,
):
    f32, bf16, i32 = jnp.float32, jnp.bfloat16, jnp.int32
    tokens, width = attended.shape
    images = tokens // P_SIZE
    embed = head_proj.shape[1]
    slots = block_ids.shape[2]
    columns = slots * BLOCK_ROWS
    cut = embed // n_dp
    dma = pltpu.SemaphoreType.DMA
    projections = gather(n_dp // 2, out_proj, head_proj)
    loss, egrad, cgrad = pl.pallas_call(
        functools.partial(main_kernel, n_dp, n_cls, images),
        name="margin_softmax",
        out_shape=(
            jax.ShapeDtypeStruct((PAD, LANES), f32),
            jax.ShapeDtypeStruct((PAD, embed), f32),
            jax.ShapeDtypeStruct((cut, class_weight.shape[0]), f32),
        ),
        in_specs=[VMEM] * 7 + [SMEM, VMEM],
        out_specs=(VMEM, VMEM, VMEM),
        scratch_shapes=[
            pltpu.VMEM((tokens, width), f32),
            pltpu.VMEM((PAD, width), bf16),
            pltpu.VMEM((n_cls, PAD, width), bf16),
            pltpu.VMEM((columns, embed), f32),
            pltpu.VMEM((embed, columns), f32),
            pltpu.VMEM((PAD, columns), f32),
            pltpu.VMEM((PAD, LANES), i32),
            pltpu.VMEM((n_dp, PAD, LANES), i32),
            pltpu.VMEM((PAD, LANES), f32),
            pltpu.VMEM((n_cls, PAD, LANES), f32),
            pltpu.VMEM((n_cls, PAD, embed), f32),
            pltpu.VMEM((n_cls, PAD, embed), f32),
            pltpu.VMEM((embed, columns), bf16),
            pltpu.VMEM((n_dp, cut, columns), bf16),
            *([dma] * 9),
            dma((n_dp,)),
            pltpu.VMEM((2, cut, class_weight.shape[0]), bf16),
            pltpu.VMEM((2, cut, class_weight.shape[0]), bf16),
            dma,
            dma((2,)),
        ],
        compiler_params=pltpu.CompilerParams(
            collective_id=1, has_side_effects=True, vmem_limit_bytes=32 << 20
        ),
    )(
        attended,
        stream,
        projections,
        class_weight,
        norm_gain.reshape(1, width),
        norm_shift.reshape(1, width),
        block_ids.reshape(1, slots),
        block_count,
        labels.reshape(1, -1),
    )
    return loss[:images, 0], egrad[:images], cgrad.T


def solution(mesh):
    n_dp, n_cls = mesh.shape["dp"], mesh.shape["cls"]
    placed = (
        P(("dp", "cls"), None),
        P(("dp", "cls"), None),
        P("dp", None),
        P(),
        P(),
        P("dp", None),
        P("cls", None),
        P("dp", "cls", None),
        P("dp", "cls"),
        P("dp"),
    )
    return jax.shard_map(
        functools.partial(per_device, n_dp, n_cls),
        mesh=mesh,
        in_specs=placed,
        out_specs=(P(("dp", "cls")), P(("dp", "cls"), None), P("cls", "dp")),
        check_vma=False,
    )
```
